32 devices in a mesh: gx: 4 (over z), gy: 4 (over y, x), gz: 2 (over core).
Axes of the slice: x: 2, y: 2, z: 4, core: 2. Of those that a mesh axis runs over, the one named last changes fastest.
Arguments:
- features: bfloat16 [8, 16, 2, 128, 256], P('gx', 'gy', 'gz'), may hold values from -6 to 6
- fractions: bfloat16 [8, 16, 2, 3, 128], P('gx', 'gy', 'gz'), may hold values from 0 to 0.98828125
- occupied: int32 [8, 16, 2, 128], P('gx', 'gy', 'gz'), may hold values 0 or 1
- wave_index: int32 [3, 512], replicated, may hold values from -14 to 14, as said below
- radial_weight: float32 [8, 4], replicated, may hold values from -4 to 4
- ewald_mix: float32 [256, 256], replicated, may hold values from -0.375 to 0.375
- msg_weight: bfloat16 [256, 256], replicated, may hold values from -0.375 to 0.375
- ewald_weight: bfloat16 [256, 256], replicated, may hold values from -0.375 to 0.375
- out_weight: bfloat16 [256, 256], replicated, may hold values from -0.375 to 0.375
Outputs:
- updated: bfloat16 [8, 16, 2, 128, 256], P('gx', 'gy', 'gz')
The draws below stay inside these ranges and needn't reach their ends.
Inputs may be any that keep to these rules, and one draw needn't show every extreme that they name: `wave_index`: no wavevector is zero, and no two wavevectors are equal or opposite.
All inputs are finite; a program needn't handle non-finite values. No bound on the sum of `occupied` on one device may be relied on, other than what follows from the above.
Results may differ from the reference program's by a relative error of at most 0.007.
Values may be sent and summed in bfloat16 or wider, within the bound.
A program may use at most 64 MiB of HBM per device.

```python
import math
import jax
import jax.numpy as jnp
from jax import lax

FEAT = 256
WAVES = 512
SLOTS = 128
HEADS = 4
BASIS = 8
NXC = 8
NYC = 16
NZC = 2
ATOMS = 32768


def draw_wave_index(key, part):
    reach_x = NXC // 2 + 6
    reach_y = NYC // 2 + 6
    reach_z = NZC // 2 + 6
    longest = max(NXC, NYC, NZC)
    factor_x = (longest // NXC) ** 2
    factor_y = (longest // NYC) ** 2
    factor_z = (longest // NZC) ** 2
    comp_x, comp_y, comp_z = jnp.meshgrid(jnp.arange(-reach_x, reach_x + 1, dtype=jnp.int32), jnp.arange(-reach_y, reach_y + 1, dtype=jnp.int32), jnp.arange(-reach_z, reach_z + 1, dtype=jnp.int32), indexing='ij')
    comp_x = comp_x.reshape(-1)
    comp_y = comp_y.reshape(-1)
    comp_z = comp_z.reshape(-1)
    upper = (comp_x > 0) | (comp_x == 0) & (comp_y > 0) | (comp_x == 0) & (comp_y == 0) & (comp_z > 0)
    norm_int = comp_x * comp_x * factor_x + comp_y * comp_y * factor_y + comp_z * comp_z * factor_z
    score = jnp.where(upper, norm_int, jnp.int32(2 ** 30))
    pool_count = score.shape[0]
    shuffled = jax.random.permutation(jax.random.fold_in(key, 31), pool_count).astype(jnp.int32)
    ranked = jnp.argsort(score[shuffled], stable=True)
    lowest = shuffled[ranked[:2 * WAVES]]
    picks = jax.random.permutation(jax.random.fold_in(key, 37), 2 * WAVES)[:WAVES]
    chosen = lowest[picks]
    signs = 2 * jax.random.randint(jax.random.fold_in(key, 41), (WAVES,), 0, 2) - 1
    values = jnp.stack([comp_x[chosen], comp_y[chosen], comp_z[chosen]], axis=0) * signs[None, :]
    return values.astype(jnp.int32)


def place_ends(entries, key, least, high):
    index_at = [jax.random.randint(jax.random.fold_in(key, axis), (), 0, length) for axis, length in enumerate(entries.shape)]
    widest = entries.shape.index(max(entries.shape))
    next_to = index_at[:widest] + [(index_at[widest] + 1) % entries.shape[widest]] + index_at[widest + 1:]
    return entries.at[tuple(index_at)].set(least).at[tuple(next_to)].set(high)


def steps_of(stream_key, shape, shards, least, high):
    loudness, own = 1.0, jax.random.fold_in(stream_key, 6)
    for position, blocks in shards:
        steps = jnp.exp(jax.random.uniform(jax.random.fold_in(own, position), (blocks,), jnp.float32, least / len(shards), high / len(shards)))
        loudness = loudness * jnp.repeat(steps, shape[position] // blocks).reshape([-1 if axis == position else 1 for axis in range(len(shape))])
    return loudness


def noise(rng, dims, scale, bound, cuts=(), kind=jnp.bfloat16):
    values = jax.random.normal(rng, dims, jnp.float32) * scale
    if len(cuts) > 0:
        values = steps_of(rng, dims, cuts, -0.22, 0.18) * values
    return jnp.clip(values, min=-bound, max=bound).astype(kind)


def setup_inputs(seed: int = 0) -> dict:
    key_of = jax.random.split(jax.random.key(seed), 10)
    return {
        "features": noise(key_of[0], (NXC, NYC, NZC, SLOTS, FEAT), 1.0, 6.0, ((0, 4), (1, 4), (2, 2))),
        "fractions": jnp.clip(0.98828125 * jax.random.uniform(key_of[1], (NXC, NYC, NZC, 3, SLOTS), jnp.float32) ** steps_of(key_of[1], (NXC, NYC, NZC, 3, SLOTS), ((0, 4), (1, 4), (2, 2)), -0.2, 0.2), 0.0, 0.98828125).astype(jnp.bfloat16),
        "occupied": place_ends((jax.random.randint(key_of[2], (NXC, NYC, NZC, SLOTS), 0, 8) < 7).astype(jnp.int32), jax.random.fold_in(key_of[2], 1), 0, 1),
        "wave_index": draw_wave_index(jax.random.fold_in(key_of[9], 71), 0),
        "radial_weight": noise(key_of[4], (BASIS, HEADS), 1.0, 4.0, (), jnp.float32),
        "ewald_mix": noise(key_of[5], (FEAT, FEAT), FEAT ** -0.5, 0.375, (), jnp.float32),
        "msg_weight": noise(key_of[6], (FEAT, FEAT), FEAT ** -0.5, 0.375),
        "ewald_weight": noise(key_of[7], (FEAT, FEAT), FEAT ** -0.5, 0.375),
        "out_weight": noise(key_of[8], (FEAT, FEAT), FEAT ** -0.5, 0.375),
    }


sharpness = 16.0
smearing = 0.04
screening = 4.0
strength = 24.0

def pair_weights(home_geom, near_geom, shift_vec, radial_weight, self_pair):
    slot_count = home_geom.shape[2]
    dist_sq = jnp.zeros((home_geom.shape[0], slot_count, slot_count), jnp.float32)
    for axis_id in range(3):
        axis_gap = near_geom[:, axis_id, None, :] + shift_vec[axis_id] - home_geom[:, axis_id, :, None]
        dist_sq = dist_sq + axis_gap * axis_gap
    distance = jnp.sqrt(dist_sq)
    envelope = jnp.square(jnp.maximum(1.0 - dist_sq, 0.0)) * near_geom[:, 3, None, :]
    envelope = envelope * (1.0 - self_pair * jnp.eye(slot_count, dtype=jnp.float32))
    level_count = radial_weight.shape[0]
    radial_sum = jnp.zeros((home_geom.shape[0], radial_weight.shape[1], slot_count, slot_count), jnp.float32)
    for level_id in range(level_count):
        radial_bump = jnp.exp(-sharpness * jnp.square(distance - level_id / (level_count - 1)))
        radial_sum = radial_sum + radial_bump[:, None] * radial_weight[level_id][None, :, None, None]
    return (radial_sum * envelope[:, None]).astype(jnp.bfloat16)

def reference(features, fractions, occupied, wave_index, radial_weight, ewald_mix, msg_weight, ewald_weight, out_weight):
    head_count = radial_weight.shape[1]
    head_width = FEAT // head_count
    plane_cells = NYC * NZC
    geometry = jnp.concatenate([fractions.astype(jnp.float32), occupied[:, :, :, None, :].astype(jnp.float32)], axis=3)
    padding = ((1, 1), (1, 1), (1, 1), (0, 0), (0, 0))
    wide_feat = jnp.pad(features, padding, mode='wrap')
    wide_geom = jnp.pad(geometry, padding, mode='wrap')
    msg_scale = 1.0 / math.sqrt(4.0 * SLOTS)
    planes = jnp.arange(NXC, dtype=jnp.int32)

    def neighbour_plane(plane_id):
        feat_slab = lax.dynamic_slice_in_dim(wide_feat, plane_id, 3, 0)
        geom_slab = lax.dynamic_slice_in_dim(wide_geom, plane_id, 3, 0)
        home_geom = lax.dynamic_index_in_dim(geometry, plane_id, 0, keepdims=False).reshape(plane_cells, 4, SLOTS)
        msg_sum = jnp.zeros((plane_cells, SLOTS, head_count, head_width), jnp.float32)
        for offset_id in range(27):
            step_x = offset_id // 9 - 1
            step_y = offset_id // 3 % 3 - 1
            step_z = offset_id % 3 - 1
            near_feat = feat_slab[step_x + 1, step_y + 1:step_y + 1 + NYC, step_z + 1:step_z + 1 + NZC]
            near_feat = near_feat.reshape(plane_cells, SLOTS, head_count, head_width)
            near_geom = geom_slab[step_x + 1, step_y + 1:step_y + 1 + NYC, step_z + 1:step_z + 1 + NZC]
            near_geom = near_geom.reshape(plane_cells, 4, SLOTS)
            shift_vec = jnp.array([step_x, step_y, step_z], jnp.float32)
            self_pair = 1.0 if offset_id == 13 else 0.0
            weights = pair_weights(home_geom, near_geom, shift_vec, radial_weight, self_pair)
            msg_sum = msg_sum + jnp.einsum('nhpq,nqhc->nphc', weights.astype(jnp.float32), near_feat.astype(jnp.float32))
        scaled = msg_sum.reshape(plane_cells, SLOTS, FEAT) * msg_scale
        return scaled.astype(jnp.bfloat16).reshape(NYC, NZC, SLOTS, FEAT)
    messages = lax.map(neighbour_plane, planes)
    lengths = jnp.array([NXC, NYC, NZC], jnp.float32)
    wave_vec = 2.0 * math.pi * wave_index.astype(jnp.float32) / lengths[:, None]
    wave_sq = lax.optimization_barrier(jnp.sum(wave_vec * wave_vec, axis=0))
    damping = strength * jnp.exp(-0.5 * smearing * wave_sq) / (wave_sq + screening) * (1.0 / math.sqrt(ATOMS * WAVES))
    y_cells = jnp.arange(NYC, dtype=jnp.int32).astype(jnp.float32)[:, None, None]
    z_cells = jnp.arange(NZC, dtype=jnp.int32).astype(jnp.float32)[None, :, None]

    def plane_basis(plane_id):
        slab = lax.dynamic_index_in_dim(fractions, plane_id, 0, keepdims=False).astype(jnp.float32)
        pos_x = plane_id.astype(jnp.float32) + slab[:, :, 0]
        pos_y = y_cells + slab[:, :, 1]
        pos_z = z_cells + slab[:, :, 2]
        phase_rows = pos_x[..., None] * wave_vec[0] + pos_y[..., None] * wave_vec[1] + pos_z[..., None] * wave_vec[2]
        phase_rows = phase_rows.reshape(plane_cells * SLOTS, WAVES)
        return jnp.concatenate([jnp.cos(phase_rows), jnp.sin(phase_rows)], axis=1).astype(jnp.bfloat16)

    def project(carry, plane_id):
        wave_basis = plane_basis(plane_id)
        plane_feat = lax.dynamic_index_in_dim(features, plane_id, 0, keepdims=False)
        plane_mask = lax.dynamic_index_in_dim(occupied, plane_id, 0, keepdims=False)
        masked = (plane_feat * plane_mask[..., None].astype(jnp.bfloat16)).reshape(plane_cells * SLOTS, FEAT)
        term = lax.dot_general(wave_basis, masked, (((0,), (0,)), ((), ())), preferred_element_type=jnp.float32)
        return (carry + term, None)
    structure, unused = lax.scan(project, jnp.zeros((2 * WAVES, FEAT), jnp.float32), planes)
    mixed_rows = jnp.dot(structure, ewald_mix, precision=lax.Precision.HIGHEST).reshape(2, WAVES, FEAT)
    filtered = (mixed_rows * damping[None, :, None]).astype(jnp.bfloat16).reshape(2 * WAVES, FEAT)

    def decode(plane_id):
        values = jnp.dot(plane_basis(plane_id), filtered, preferred_element_type=jnp.float32)
        return values.astype(jnp.bfloat16).reshape(NYC, NZC, SLOTS, FEAT)
    ewald_out = lax.map(decode, planes)
    msg_rows = messages.reshape(-1, FEAT)
    ewald_rows = ewald_out.reshape(-1, FEAT)
    joined = jnp.dot(msg_rows, msg_weight, preferred_element_type=jnp.float32) + jnp.dot(ewald_rows, ewald_weight, preferred_element_type=jnp.float32)
    hidden = jax.nn.silu(joined).astype(jnp.bfloat16)
    result = features.reshape(-1, FEAT).astype(jnp.float32) + jnp.dot(hidden, out_weight, preferred_element_type=jnp.float32)
    result = result * occupied.reshape(-1, 1).astype(jnp.float32)
    return result.astype(jnp.bfloat16).reshape(features.shape)
```

```python
import functools
import math

import jax
import jax.numpy as jnp
from jax import lax
from jax.experimental import pallas as pl
from jax.experimental.pallas import tpu as pltpu
from jax.sharding import PartitionSpec as P

sharpness = 16.0
smearing = 0.04
screening = 4.0
strength = 24.0

SIN_C = [(-1.0) ** k * math.pi ** (2 * k + 1) / math.factorial(2 * k + 1) for k in range(7)]
COS_C = [(-1.0) ** k * math.pi ** (2 * k) / math.factorial(2 * k) for k in range(7)]


def poly(z, coefs):
    acc = jnp.full_like(z, coefs[-1])
    for c in coefs[-2::-1]:
        acc = acc * z + c
    return acc


def shifted(x, axis, dim, width):
    count, length = lax.axis_size(axis), x.shape[dim]
    up = [(i, (i + 1) % count) for i in range(count)]
    down = [(j, i) for i, j in up]
    last = lax.slice_in_dim(x, length - width, length, axis=dim)
    first = lax.slice_in_dim(x, 0, width, axis=dim)
    return lax.ppermute(last, axis, up), lax.ppermute(first, axis, down)


def widen(x, axis, dim):
    before, after = shifted(x, axis, dim, 1)
    return jnp.concatenate([before, x, after], axis=dim)


def message_kernel(cells_y, cells_z, fold_z, levels, home_ref, feat_ref, geom_ref, wb_ref, out_ref, hb, phi, acc):
    cell = pl.program_id(0)
    x = cell // (cells_y * cells_z)
    y = (cell // cells_z) % cells_y
    z = cell % cells_z
    slots = out_ref.shape[1]
    feat = out_ref.shape[2]
    near_z = feat_ref.shape[3]
    chunk = 32
    for a in range(3):
        hb[a] = jnp.broadcast_to(home_ref[0, :, a : a + 1], (slots, slots))
    for ox in range(3):
        for oy in range(3):
            for oz in range(near_z):
                g = geom_ref[x + ox, z, y + oy, oz]
                nx = g[0:1] + (ox - 1.0)
                ny = g[1:2] + (oy - 1.0)
                if fold_z:
                    nz = g[2:3]
                else:
                    nz = g[2:3] + (oz - 1.0)
                col = (oy * near_z + oz) * slots
                center = ox == 1 and oy == 1 and oz == (0 if fold_z else 1)
                for p0 in range(0, slots, chunk):
                    dx = nx - hb[0, p0 : p0 + chunk]
                    dy = ny - hb[1, p0 : p0 + chunk]
                    dz = nz - hb[2, p0 : p0 + chunk]
                    if fold_z and oz == 1:
                        dz = 1.0 - jnp.abs(dz)
                    sq = jnp.minimum(dx * dx + dy * dy + dz * dz, 1.0)
                    dist = sq * lax.rsqrt(jnp.maximum(sq, 1e-30))
                    ratio = jnp.exp2(dist * (2.0 * sharpness / (levels - 1) * math.log2(math.e)))
                    edge = 1.0 - sq
                    val = edge * edge * jnp.exp2(sq * (-sharpness * math.log2(math.e)))
                    if center:
                        row = lax.broadcasted_iota(jnp.int32, val.shape, 0) + p0
                        lane = lax.broadcasted_iota(jnp.int32, val.shape, 1)
                        val = jnp.where(row == lane, 0.0, val)
                    for b in range(levels):
                        phi[ox, b * slots + p0 : b * slots + p0 + chunk, col : col + slots] = val.astype(jnp.bfloat16)
                        if b + 1 < levels:
                            val = val * ratio
        rows = feat_ref[x + ox, z, pl.ds(y, 3)].reshape(3 * near_z * slots, feat)
        part = jnp.dot(phi[ox], rows, preferred_element_type=jnp.float32)
        if ox == 0:
            acc[...] = part
        elif ox == 1:
            acc[...] += part
    total = jnp.zeros((slots, feat), jnp.float32)
    for b in range(levels):
        both = acc[b * slots : (b + 1) * slots] + part[b * slots : (b + 1) * slots]
        total = total + both * wb_ref[b : b + 1]
    out_ref[0] = total.astype(jnp.bfloat16)


def basis_kernel(pos_ref, wave_ref, feat_ref, basis_ref, struct_ref):
    cell = pl.program_id(0)
    waves = wave_ref.shape[0]
    pos = pos_ref[0]
    chunk = 64
    for w0 in range(0, waves, chunk):
        wv = wave_ref[w0 : w0 + chunk]
        turns = wv[:, 0:1] * pos[0:1] + wv[:, 1:2] * pos[1:2] + wv[:, 2:3] * pos[2:3]
        u = turns - jnp.floor(turns + 0.5)
        q = u * u
        s = u * poly(q, SIN_C)
        c = poly(q, COS_C)
        basis_ref[0, w0 : w0 + chunk] = (1.0 - 2.0 * s * s).astype(jnp.bfloat16)
        basis_ref[0, waves + w0 : waves + w0 + chunk] = (2.0 * s * c).astype(jnp.bfloat16)
    part = jnp.dot(basis_ref[0], feat_ref[0], preferred_element_type=jnp.float32)

    @pl.when(cell == 0)
    def _():
        struct_ref[...] = part

    @pl.when(cell > 0)
    def _():
        struct_ref[...] += part


def final_kernel(basis_ref, grid_ref, msg_ref, feat_ref, home_ref, wm_ref, wo_ref, out_ref):
    far = lax.dot_general(
        basis_ref[0], grid_ref[...], (((0,), (0,)), ((), ())), preferred_element_type=jnp.float32
    )
    joined = far + jnp.dot(msg_ref[0], wm_ref[...], preferred_element_type=jnp.float32)
    hidden = (joined / (1.0 + jnp.exp(-joined))).astype(jnp.bfloat16)
    result = feat_ref[0].astype(jnp.float32) + jnp.dot(hidden, wo_ref[...], preferred_element_type=jnp.float32)
    out_ref[0] = (result * home_ref[0, :, 3:4]).astype(jnp.bfloat16)


def body(
    features,
    fractions,
    occupied,
    wave_index,
    radial_weight,
    ewald_mix,
    msg_weight,
    ewald_weight,
    out_weight,
):
    cx, cy, cz, slots, feat = features.shape
    levels, heads = radial_weight.shape
    cells = cx * cy * cz
    grid = [lax.axis_size("gx") * cx, lax.axis_size("gy") * cy, lax.axis_size("gz") * cz]
    devices = lax.axis_size("gx") * lax.axis_size("gy") * lax.axis_size("gz")
    waves = wave_index.shape[1]
    axes = ("gx", "gy", "gz")
    full = lambda shape: pl.BlockSpec(shape, lambda i: (0,) * len(shape))
    params = pltpu.CompilerParams(dimension_semantics=("arbitrary",), vmem_limit_bytes=56 * 2**20)

    masked = features * occupied[..., None].astype(jnp.bfloat16)
    frac = fractions.astype(jnp.float32)
    cell_feat = masked.reshape(cells, slots, feat)
    home = jnp.concatenate([frac, occupied[:, :, :, None, :].astype(jnp.float32)], axis=3)
    home = jnp.swapaxes(home.reshape(cells, 4, slots), 1, 2)

    start = [
        (lax.axis_index(n) * c + jnp.arange(c, dtype=jnp.int32)).astype(jnp.float32)
        for n, c in zip(axes, (cx, cy, cz))
    ]
    origin = jnp.stack(jnp.meshgrid(*start, indexing="ij"), axis=-1)[..., None]
    pos = (origin + frac).reshape(cells, 3, slots)
    lengths = jnp.array(grid, jnp.float32)
    index = wave_index.astype(jnp.float32)
    wave_vec = 2.0 * math.pi * index / lengths[:, None]
    wave_sq = jnp.sum(wave_vec * wave_vec, axis=0)
    damping = (
        strength
        * jnp.exp(-0.5 * smearing * wave_sq)
        / (wave_sq + screening)
        * (1.0 / math.sqrt(cells * slots * devices * waves))
    )
    wave_turn = (index / lengths[:, None]).T

    basis, struct = pl.pallas_call(
        basis_kernel,
        grid=(cells,),
        in_specs=[
            pl.BlockSpec((1, 3, slots), lambda i: (i, 0, 0)),
            full((waves, 3)),
            pl.BlockSpec((1, slots, feat), lambda i: (i, 0, 0)),
        ],
        out_specs=[pl.BlockSpec((1, 2 * waves, slots), lambda i: (i, 0, 0)), full((2 * waves, feat))],
        out_shape=[
            jax.ShapeDtypeStruct((cells, 2 * waves, slots), jnp.bfloat16),
            jax.ShapeDtypeStruct((2 * waves, feat), jnp.float32),
        ],
        compiler_params=params,
        name="basis",
    )(pos, wave_turn, cell_feat)

    wave_share = lax.psum_scatter(struct.reshape(2, waves, feat), axes, scatter_dimension=1, tiled=True)
    share_rows = wave_share.shape[1]
    share_damp = lax.dynamic_slice_in_dim(damping, lax.axis_index(axes) * share_rows, share_rows, 0)
    mixed = jnp.dot(wave_share.reshape(2 * share_rows, feat), ewald_mix, precision=lax.Precision.HIGHEST)
    filtered = (mixed.reshape(2, share_rows, feat) * share_damp[None, :, None]).astype(jnp.bfloat16)
    projected = jnp.dot(filtered, ewald_weight, preferred_element_type=jnp.float32).astype(jnp.bfloat16)
    field = lax.all_gather(projected, axes, axis=1, tiled=True).reshape(2 * waves, feat)

    fold_z = grid[2] == 2 and cz == 1
    wide_feat = widen(widen(masked, "gx", 0), "gy", 1)
    wide_geom = widen(widen(fractions, "gx", 0), "gy", 1)
    if fold_z:
        swap = [(0, 1), (1, 0)]
        wide_feat = jnp.concatenate([wide_feat, lax.ppermute(wide_feat, "gz", swap)], axis=2)
        wide_geom = jnp.concatenate([wide_geom, lax.ppermute(wide_geom, "gz", swap)], axis=2)
        near_z = 2
    else:
        wide_feat = widen(wide_feat, "gz", 2)
        wide_geom = widen(wide_geom, "gz", 2)
        near_z = 3
    wide_feat = jnp.stack([wide_feat[:, :, z : z + near_z] for z in range(cz)], axis=1)
    wide_geom = jnp.stack([wide_geom[:, :, z : z + near_z] for z in range(cz)], axis=1).astype(jnp.float32)
    level = jnp.arange(levels, dtype=jnp.float32) / (levels - 1)
    wb = radial_weight * (jnp.exp(-sharpness * level * level) / math.sqrt(4.0 * slots))[:, None]
    wb = jnp.repeat(wb, feat // heads, axis=1)
    messages = pl.pallas_call(
        functools.partial(message_kernel, cy, cz, fold_z, levels),
        grid=(cells,),
        in_specs=[
            pl.BlockSpec((1, slots, 4), lambda i: (i, 0, 0)),
            full(wide_feat.shape),
            full(wide_geom.shape),
            full(wb.shape),
        ],
        out_specs=pl.BlockSpec((1, slots, feat), lambda i: (i, 0, 0)),
        out_shape=jax.ShapeDtypeStruct((cells, slots, feat), jnp.bfloat16),
        scratch_shapes=[
            pltpu.VMEM((3, slots, slots), jnp.float32),
            pltpu.VMEM((3, levels * slots, 3 * near_z * slots), jnp.bfloat16),
            pltpu.VMEM((levels * slots, feat), jnp.float32),
        ],
        compiler_params=params,
        cost_estimate=pl.CostEstimate(
            flops=2 * cells * levels * slots * 9 * near_z * slots * feat, bytes_accessed=2**22, transcendentals=0
        ),
        name="messages",
    )(home, wide_feat, wide_geom, wb)

    out = pl.pallas_call(
        final_kernel,
        grid=(cells,),
        in_specs=[
            pl.BlockSpec((1, 2 * waves, slots), lambda i: (i, 0, 0)),
            full((2 * waves, feat)),
            pl.BlockSpec((1, slots, feat), lambda i: (i, 0, 0)),
            pl.BlockSpec((1, slots, feat), lambda i: (i, 0, 0)),
            pl.BlockSpec((1, slots, 4), lambda i: (i, 0, 0)),
            full((feat, feat)),
            full((feat, feat)),
        ],
        out_specs=pl.BlockSpec((1, slots, feat), lambda i: (i, 0, 0)),
        out_shape=jax.ShapeDtypeStruct((cells, slots, feat), jnp.bfloat16),
        compiler_params=params,
        name="final",
    )(basis, field, messages, cell_feat, home, msg_weight, out_weight)
    return out.reshape(features.shape)


def solution(mesh):
    cell = P("gx", "gy", "gz", None, None)
    in_specs = (cell, cell, P("gx", "gy", "gz", None), P(), P(), P(), P(), P(), P())
    return jax.shard_map(body, mesh=mesh, in_specs=in_specs, out_specs=cell, check_vma=False)
```

```python
import functools
import math

import jax
import jax.numpy as jnp
from jax import lax
from jax.experimental import pallas as pl
from jax.experimental.pallas import tpu as pltpu
from jax.sharding import PartitionSpec as P

sharpness = 16.0
smearing = 0.04
screening = 4.0
strength = 24.0

SIN_C = [(-1.0) ** k * math.pi ** (2 * k + 1) / math.factorial(2 * k + 1) for k in range(7)]
COS_C = [(-1.0) ** k * math.pi ** (2 * k) / math.factorial(2 * k) for k in range(7)]


def poly(z, coefs):
    acc = jnp.full_like(z, coefs[-1])
    for c in coefs[-2::-1]:
        acc = acc * z + c
    return acc


def shifted(x, axis, dim, width):
    count, length = lax.axis_size(axis), x.shape[dim]
    up = [(i, (i + 1) % count) for i in range(count)]
    down = [(j, i) for i, j in up]
    last = lax.slice_in_dim(x, length - width, length, axis=dim)
    first = lax.slice_in_dim(x, 0, width, axis=dim)
    return lax.ppermute(last, axis, up), lax.ppermute(first, axis, down)


def widen(x, axis, dim):
    before, after = shifted(x, axis, dim, 1)
    return jnp.concatenate([before, x, after], axis=dim)


def message_kernel(cells_y, cells_z, fold_z, levels, home_ref, feat_ref, geom_ref, wb_ref, out_ref, hb, phi, acc):
    cell = pl.program_id(0)
    x = cell // (cells_y * cells_z)
    y = (cell // cells_z) % cells_y
    z = cell % cells_z
    slots = out_ref.shape[1]
    feat = out_ref.shape[2]
    near_z = feat_ref.shape[3]
    chunk = 32
    for a in range(3):
        hb[a] = jnp.broadcast_to(home_ref[0, :, a : a + 1], (slots, slots))
    for ox in range(3):
        for oy in range(3):
            for oz in range(near_z):
                g = geom_ref[x + ox, z, y + oy, oz]
                nx = g[0:1] + (ox - 1.0)
                ny = g[1:2] + (oy - 1.0)
                if fold_z:
                    nz = g[2:3]
                else:
                    nz = g[2:3] + (oz - 1.0)
                col = (oy * near_z + oz) * slots
                center = ox == 1 and oy == 1 and oz == (0 if fold_z else 1)
                for p0 in range(0, slots, chunk):
                    dx = nx - hb[0, p0 : p0 + chunk]
                    dy = ny - hb[1, p0 : p0 + chunk]
                    dz = nz - hb[2, p0 : p0 + chunk]
                    if fold_z and oz == 1:
                        dz = 1.0 - jnp.abs(dz)
                    radial_terms(dx, dy, dz, levels, center, p0, phi.at[ox], col, slots)
        rows = feat_ref[x + ox, z, pl.ds(y, 3)].reshape(3 * near_z * slots, feat)
        part = jnp.dot(phi[ox], rows, preferred_element_type=jnp.float32)
        if ox == 0:
            acc[...] = part
        elif ox == 1:
            acc[...] += part
    total = jnp.zeros((slots, feat), jnp.float32)
    for b in range(levels):
        both = acc[b * slots : (b + 1) * slots] + part[b * slots : (b + 1) * slots]
        total = total + both * wb_ref[b : b + 1]
    out_ref[0] = total.astype(jnp.bfloat16)


def basis_kernel(pos_ref, wave_ref, feat_ref, basis_ref, struct_ref):
    cell = pl.program_id(0)
    waves = wave_ref.shape[0]
    pos = pos_ref[0]
    chunk = 64
    for w0 in range(0, waves, chunk):
        wv = wave_ref[w0 : w0 + chunk]
        turns = wv[:, 0:1] * pos[0:1] + wv[:, 1:2] * pos[1:2] + wv[:, 2:3] * pos[2:3]
        u = turns - jnp.floor(turns + 0.5)
        q = u * u
        s = u * poly(q, SIN_C)
        c = poly(q, COS_C)
        basis_ref[0, w0 : w0 + chunk] = (1.0 - 2.0 * s * s).astype(jnp.bfloat16)
        basis_ref[0, waves + w0 : waves + w0 + chunk] = (2.0 * s * c).astype(jnp.bfloat16)
    part = jnp.dot(basis_ref[0], feat_ref[0], preferred_element_type=jnp.float32)

    @pl.when(cell == 0)
    def _():
        struct_ref[...] = part

    @pl.when(cell > 0)
    def _():
        struct_ref[...] += part


def final_kernel(basis_ref, grid_ref, msg_ref, feat_ref, home_ref, wm_ref, wo_ref, out_ref):
    far = lax.dot_general(
        basis_ref[0], grid_ref[...], (((0,), (0,)), ((), ())), preferred_element_type=jnp.float32
    )
    joined = far + jnp.dot(msg_ref[0], wm_ref[...], preferred_element_type=jnp.float32)
    hidden = (joined / (1.0 + jnp.exp(-joined))).astype(jnp.bfloat16)
    result = feat_ref[0].astype(jnp.float32) + jnp.dot(hidden, wo_ref[...], preferred_element_type=jnp.float32)
    out_ref[0] = (result * home_ref[0, :, 3:4]).astype(jnp.bfloat16)


def coords(index, counts):
    return (index // (counts[1] * counts[2]), (index // counts[2]) % counts[1], index % counts[2])


def layer_kernel(
    counts,
    levels,
    pack_ref,
    home_ref,
    pos_ref,
    wave_ref,
    wb_ref,
    damp_ref,
    mix_ref,
    we_ref,
    wm_ref,
    wo_ref,
    out_ref,
    wide,
    hb,
    phi,
    acc,
    basis,
    struct,
    parts,
    share,
    field,
    msg,
    halo_send,
    halo_recv,
    own_sem,
    part_send,
    part_recv,
    share_send,
    share_recv,
):
    cx, cy = pack_ref.shape[0], pack_ref.shape[1]
    cells, slots, feat = out_ref.shape
    waves = wave_ref.shape[0]
    devices = counts[0] * counts[1] * counts[2]
    rows = waves // devices
    at = (lax.axis_index("gx"), lax.axis_index("gy"), lax.axis_index("gz"))
    me = (at[0] * counts[1] + at[1]) * counts[2] + at[2]
    mesh_id = pl.DeviceIdType.MESH

    barrier = pltpu.get_barrier_semaphore()

    @pl.loop(1, devices)
    def _(k):
        pl.semaphore_signal(barrier, inc=1, device_id=coords((me + k) % devices, counts), device_id_type=mesh_id)

    pl.semaphore_wait(barrier, devices - 1)

    own = pltpu.make_async_copy(pack_ref, wide.at[pl.ds(1, cx), pl.ds(1, cy), 0], own_sem)
    own.start()

    def span(step, length):
        if step == 0:
            return 0, 1, length
        if step == 1:
            return length - 1, 0, 1
        return 0, length + 1, 1

    halo = []
    for dx in (1, -1, 0):
        for dy in (1, -1, 0):
            for dz in (0, 1):
                if (dx, dy, dz) == (0, 0, 0):
                    continue
                sx, tx, lx = span(dx, cx)
                sy, ty, ly = span(dy, cy)
                target = (
                    (at[0] + dx + counts[0]) % counts[0],
                    (at[1] + dy + counts[1]) % counts[1],
                    (at[2] + dz) % counts[2],
                )
                copy = pltpu.make_async_remote_copy(
                    src_ref=pack_ref.at[pl.ds(sx, lx), pl.ds(sy, ly)],
                    dst_ref=wide.at[pl.ds(tx, lx), pl.ds(ty, ly), dz],
                    send_sem=halo_send.at[len(halo)],
                    recv_sem=halo_recv.at[len(halo)],
                    device_id=target,
                    device_id_type=mesh_id,
                )
                copy.start()
                halo.append(copy)

    @pl.loop(0, cells)
    def _(cell):
        pos = pos_ref[cell]
        lanes = pl.ds(pl.multiple_of(cell * slots, slots), slots)
        chunk = 64
        for w0 in range(0, waves, chunk):
            wv = wave_ref[w0 : w0 + chunk]
            turns = wv[:, 0:1] * pos[0:1] + wv[:, 1:2] * pos[1:2] + wv[:, 2:3] * pos[2:3]
            u = turns - jnp.floor(turns + 0.5)
            q = u * u
            s = u * poly(q, SIN_C)
            c = poly(q, COS_C)
            basis[w0 : w0 + chunk, lanes] = (1.0 - 2.0 * s * s).astype(jnp.bfloat16)
            basis[waves + w0 : waves + w0 + chunk, lanes] = (2.0 * s * c).astype(jnp.bfloat16)

    atoms = pack_ref[:, :, 0:slots, :].reshape(cells * slots, feat)
    struct[...] = (
        jnp.dot(basis[...], atoms, preferred_element_type=jnp.float32)
        .astype(jnp.bfloat16)
        .reshape(2, devices, rows, feat)
    )

    def part_copy(k):
        peer = (me + k) % devices
        return pltpu.make_async_remote_copy(
            src_ref=struct.at[:, peer],
            dst_ref=parts.at[k],
            send_sem=part_send.at[k],
            recv_sem=part_recv.at[k],
            device_id=coords(peer, counts),
            device_id_type=mesh_id,
        )

    def share_copy(k, slot):
        return pltpu.make_async_remote_copy(
            src_ref=share,
            dst_ref=field.at[:, slot],
            send_sem=share_send.at[k],
            recv_sem=share_recv.at[k],
            device_id=coords((me + k) % devices, counts),
            device_id_type=mesh_id,
        )

    @pl.loop(1, devices)
    def _(k):
        part_copy(k).start()

    own.wait()
    for copy in halo:
        copy.wait()

    @pl.loop(0, cells)
    def _(cell):
        @pl.when(cell == cells // 2)
        def _():
            @pl.loop(1, devices)
            def _(k):
                part_copy(k).wait()

            parts[0] = struct[:, me]
            total = jnp.sum(parts[...].astype(jnp.float32), axis=0).reshape(2 * rows, feat)
            mixed = jnp.dot(total, mix_ref[...], precision=lax.Precision.HIGHEST, preferred_element_type=jnp.float32)
            filtered = (mixed * damp_ref[...]).astype(jnp.bfloat16)
            projected = jnp.dot(filtered, we_ref[...], preferred_element_type=jnp.float32)
            projected = projected.astype(jnp.bfloat16).reshape(2, rows, feat)
            share[...] = projected
            field[:, me] = projected

            @pl.loop(1, devices)
            def _(k):
                share_copy(k, me).start()

        x = cell // cy
        y = cell % cy
        for a in range(3):
            hb[a] = jnp.broadcast_to(home_ref[cell, :, a : a + 1], (slots, slots))
        chunk = 32
        for ox in range(3):
            for oy in range(3):
                for oz in range(2):
                    g = wide[x + ox, y + oy, oz, slots : slots + 16, 0:slots].astype(jnp.float32)
                    nx = g[0:1] + (ox - 1.0)
                    ny = g[1:2] + (oy - 1.0)
                    nz = g[2:3]
                    col = (oy * 2 + oz) * slots
                    for p0 in range(0, slots, chunk):
                        gx = nx - hb[0, p0 : p0 + chunk]
                        gy = ny - hb[1, p0 : p0 + chunk]
                        gz = nz - hb[2, p0 : p0 + chunk]
                        if oz == 1:
                            gz = 1.0 - jnp.abs(gz)
                        radial_terms(gx, gy, gz, levels, (ox, oy, oz) == (1, 1, 0), p0, phi.at[ox], col, slots)
            near = wide[x + ox, pl.ds(y, 3), :, 0:slots].reshape(6 * slots, feat)
            part = jnp.dot(phi[ox], near, preferred_element_type=jnp.float32)
            if ox == 0:
                acc[...] = part
            elif ox == 1:
                acc[...] += part
        total = jnp.zeros((slots, feat), jnp.float32)
        for b in range(levels):
            both = acc[b * slots : (b + 1) * slots] + part[b * slots : (b + 1) * slots]
            total = total + both * wb_ref[b : b + 1]
        msg[cell] = total.astype(jnp.bfloat16)

    @pl.loop(1, devices)
    def _(k):
        share_copy(k, (me - k + devices) % devices).wait()

    waves_field = field[...].reshape(2 * waves, feat)

    @pl.loop(0, cells)
    def _(cell):
        lanes = pl.ds(pl.multiple_of(cell * slots, slots), slots)
        far = lax.dot_general(
            basis[:, lanes], waves_field, (((0,), (0,)), ((), ())), preferred_element_type=jnp.float32
        )
        joined = far + jnp.dot(msg[cell], wm_ref[...], preferred_element_type=jnp.float32)
        hidden = (joined / (1.0 + jnp.exp(-joined))).astype(jnp.bfloat16)
        atom = pack_ref[cell // cy, cell % cy, 0:slots].astype(jnp.float32)
        result = atom + jnp.dot(hidden, wo_ref[...], preferred_element_type=jnp.float32)
        out_ref[cell] = (result * home_ref[cell, :, 3:4]).astype(jnp.bfloat16)


def radial_terms(gx, gy, gz, levels, center, p0, phi, col, slots):
    rows = gx.shape[0]
    sq = jnp.minimum(gx * gx + gy * gy + gz * gz, 1.0)
    dist = sq * lax.rsqrt(jnp.maximum(sq, 1e-30))
    ratio = jnp.exp2(dist * (2.0 * sharpness / (levels - 1) * math.log2(math.e)))
    edge = 1.0 - sq
    val = edge * edge * jnp.exp2(sq * (-sharpness * math.log2(math.e)))
    if center:
        row = lax.broadcasted_iota(jnp.int32, val.shape, 0) + p0
        lane = lax.broadcasted_iota(jnp.int32, val.shape, 1)
        val = jnp.where(row == lane, 0.0, val)
    for b in range(levels):
        phi[b * slots + p0 : b * slots + p0 + rows, col : col + slots] = val.astype(jnp.bfloat16)
        if b + 1 < levels:
            val = val * ratio


def body(
    features,
    fractions,
    occupied,
    wave_index,
    radial_weight,
    ewald_mix,
    msg_weight,
    ewald_weight,
    out_weight,
):
    cx, cy, cz, slots, feat = features.shape
    levels, heads = radial_weight.shape
    cells = cx * cy * cz
    grid = [lax.axis_size("gx") * cx, lax.axis_size("gy") * cy, lax.axis_size("gz") * cz]
    devices = lax.axis_size("gx") * lax.axis_size("gy") * lax.axis_size("gz")
    waves = wave_index.shape[1]
    axes = ("gx", "gy", "gz")
    full = lambda shape: pl.BlockSpec(shape, lambda i: (0,) * len(shape))
    params = pltpu.CompilerParams(dimension_semantics=("arbitrary",), vmem_limit_bytes=56 * 2**20)

    masked = features * occupied[..., None].astype(jnp.bfloat16)
    frac = fractions.astype(jnp.float32)
    cell_feat = masked.reshape(cells, slots, feat)
    home = jnp.concatenate([frac, occupied[:, :, :, None, :].astype(jnp.float32)], axis=3)
    home = jnp.swapaxes(home.reshape(cells, 4, slots), 1, 2)

    start = [
        (lax.axis_index(n) * c + jnp.arange(c, dtype=jnp.int32)).astype(jnp.float32)
        for n, c in zip(axes, (cx, cy, cz))
    ]
    origin = jnp.stack(jnp.meshgrid(*start, indexing="ij"), axis=-1)[..., None]
    pos = (origin + frac).reshape(cells, 3, slots)
    lengths = jnp.array(grid, jnp.float32)
    index = wave_index.astype(jnp.float32)
    wave_vec = 2.0 * math.pi * index / lengths[:, None]
    wave_sq = jnp.sum(wave_vec * wave_vec, axis=0)
    damping = (
        strength
        * jnp.exp(-0.5 * smearing * wave_sq)
        / (wave_sq + screening)
        * (1.0 / math.sqrt(cells * slots * devices * waves))
    )
    wave_turn = (index / lengths[:, None]).T

    fold_z = grid[2] == 2 and cz == 1
    level = jnp.arange(levels, dtype=jnp.float32) / (levels - 1)
    wb = radial_weight * (jnp.exp(-sharpness * level * level) / math.sqrt(4.0 * slots))[:, None]
    wb = jnp.repeat(wb, feat // heads, axis=1)
    counts = tuple(lax.axis_size(n) for n in axes)
    rows = waves // devices
    if fold_z and rows % 16 == 0 and min(counts) > 1:
        spread = jnp.pad(fractions, ((0, 0),) * 3 + ((0, 13), (0, feat - slots)))
        pack = jnp.concatenate([masked, spread], axis=3).reshape(cx, cy, slots + 16, feat)
        damp = lax.dynamic_slice_in_dim(damping, lax.axis_index(axes) * rows, rows, 0)
        damp = jnp.concatenate([damp, damp]).reshape(2 * rows, 1)
        vmem = pl.BlockSpec(memory_space=pltpu.VMEM)
        dma = pltpu.SemaphoreType.DMA
        out = pl.pallas_call(
            functools.partial(layer_kernel, counts, levels),
            in_specs=[vmem] * 10,
            out_specs=vmem,
            out_shape=jax.ShapeDtypeStruct((cells, slots, feat), jnp.bfloat16),
            scratch_shapes=[
                pltpu.VMEM((cx + 2, cy + 2, 2, slots + 16, feat), jnp.bfloat16),
                pltpu.VMEM((3, slots, slots), jnp.float32),
                pltpu.VMEM((3, levels * slots, 6 * slots), jnp.bfloat16),
                pltpu.VMEM((levels * slots, feat), jnp.float32),
                pltpu.VMEM((2 * waves, cells * slots), jnp.bfloat16),
                pltpu.VMEM((2, devices, rows, feat), jnp.bfloat16),
                pltpu.VMEM((devices, 2, rows, feat), jnp.bfloat16),
                pltpu.VMEM((2, rows, feat), jnp.bfloat16),
                pltpu.VMEM((2, devices, rows, feat), jnp.bfloat16),
                pltpu.VMEM((cells, slots, feat), jnp.bfloat16),
                dma((17,)),
                dma((17,)),
                dma,
                dma((devices,)),
                dma((devices,)),
                dma((devices,)),
                dma((devices,)),
            ],
            compiler_params=pltpu.CompilerParams(
                collective_id=0, has_side_effects=True, vmem_limit_bytes=56 * 2**20
            ),
            name="layer",
        )(pack, home, pos, wave_turn, wb, damp, ewald_mix, ewald_weight, msg_weight, out_weight)
        return out.reshape(features.shape)

    basis, struct = pl.pallas_call(
        basis_kernel,
        grid=(cells,),
        in_specs=[
            pl.BlockSpec((1, 3, slots), lambda i: (i, 0, 0)),
            full((waves, 3)),
            pl.BlockSpec((1, slots, feat), lambda i: (i, 0, 0)),
        ],
        out_specs=[pl.BlockSpec((1, 2 * waves, slots), lambda i: (i, 0, 0)), full((2 * waves, feat))],
        out_shape=[
            jax.ShapeDtypeStruct((cells, 2 * waves, slots), jnp.bfloat16),
            jax.ShapeDtypeStruct((2 * waves, feat), jnp.float32),
        ],
        compiler_params=params,
        name="basis",
    )(pos, wave_turn, cell_feat)

    wave_share = lax.psum_scatter(struct.reshape(2, waves, feat), axes, scatter_dimension=1, tiled=True)
    share_rows = wave_share.shape[1]
    share_damp = lax.dynamic_slice_in_dim(damping, lax.axis_index(axes) * share_rows, share_rows, 0)
    mixed = jnp.dot(wave_share.reshape(2 * share_rows, feat), ewald_mix, precision=lax.Precision.HIGHEST)
    filtered = (mixed.reshape(2, share_rows, feat) * share_damp[None, :, None]).astype(jnp.bfloat16)
    projected = jnp.dot(filtered, ewald_weight, preferred_element_type=jnp.float32).astype(jnp.bfloat16)
    field = lax.all_gather(projected, axes, axis=1, tiled=True).reshape(2 * waves, feat)

    wide_feat = widen(widen(masked, "gx", 0), "gy", 1)
    wide_geom = widen(widen(fractions, "gx", 0), "gy", 1)
    if fold_z:
        swap = [(0, 1), (1, 0)]
        wide_feat = jnp.concatenate([wide_feat, lax.ppermute(wide_feat, "gz", swap)], axis=2)
        wide_geom = jnp.concatenate([wide_geom, lax.ppermute(wide_geom, "gz", swap)], axis=2)
        near_z = 2
    else:
        wide_feat = widen(wide_feat, "gz", 2)
        wide_geom = widen(wide_geom, "gz", 2)
        near_z = 3
    wide_feat = jnp.stack([wide_feat[:, :, z : z + near_z] for z in range(cz)], axis=1)
    wide_geom = jnp.stack([wide_geom[:, :, z : z + near_z] for z in range(cz)], axis=1).astype(jnp.float32)
    messages = pl.pallas_call(
        functools.partial(message_kernel, cy, cz, fold_z, levels),
        grid=(cells,),
        in_specs=[
            pl.BlockSpec((1, slots, 4), lambda i: (i, 0, 0)),
            full(wide_feat.shape),
            full(wide_geom.shape),
            full(wb.shape),
        ],
        out_specs=pl.BlockSpec((1, slots, feat), lambda i: (i, 0, 0)),
        out_shape=jax.ShapeDtypeStruct((cells, slots, feat), jnp.bfloat16),
        scratch_shapes=[
            pltpu.VMEM((3, slots, slots), jnp.float32),
            pltpu.VMEM((3, levels * slots, 3 * near_z * slots), jnp.bfloat16),
            pltpu.VMEM((levels * slots, feat), jnp.float32),
        ],
        compiler_params=params,
        cost_estimate=pl.CostEstimate(
            flops=2 * cells * levels * slots * 9 * near_z * slots * feat, bytes_accessed=2**22, transcendentals=0
        ),
        name="messages",
    )(home, wide_feat, wide_geom, wb)

    out = pl.pallas_call(
        final_kernel,
        grid=(cells,),
        in_specs=[
            pl.BlockSpec((1, 2 * waves, slots), lambda i: (i, 0, 0)),
            full((2 * waves, feat)),
            pl.BlockSpec((1, slots, feat), lambda i: (i, 0, 0)),
            pl.BlockSpec((1, slots, feat), lambda i: (i, 0, 0)),
            pl.BlockSpec((1, slots, 4), lambda i: (i, 0, 0)),
            full((feat, feat)),
            full((feat, feat)),
        ],
        out_specs=pl.BlockSpec((1, slots, feat), lambda i: (i, 0, 0)),
        out_shape=jax.ShapeDtypeStruct((cells, slots, feat), jnp.bfloat16),
        compiler_params=params,
        name="final",
    )(basis, field, messages, cell_feat, home, msg_weight, out_weight)
    return out.reshape(features.shape)


def solution(mesh):
    cell = P("gx", "gy", "gz", None, None)
    in_specs = (cell, cell, P("gx", "gy", "gz", None), P(), P(), P(), P(), P(), P())
    return jax.shard_map(body, mesh=mesh, in_specs=in_specs, out_specs=cell, check_vma=False)
```

```python
import functools
import math

import jax
import jax.numpy as jnp
from jax import lax
from jax.experimental import pallas as pl
from jax.experimental.pallas import tpu as pltpu
from jax.sharding import PartitionSpec as P

sharpness = 16.0
smearing = 0.04
screening = 4.0
strength = 24.0

SIN_C = [(-1.0) ** k * math.pi ** (2 * k + 1) / math.factorial(2 * k + 1) for k in range(7)]
COS_C = [(-1.0) ** k * math.pi ** (2 * k) / math.factorial(2 * k) for k in range(7)]


def poly(z, coefs):
    acc = jnp.full_like(z, coefs[-1])
    for c in coefs[-2::-1]:
        acc = acc * z + c
    return acc


def shifted(x, axis, dim, width):
    count, length = lax.axis_size(axis), x.shape[dim]
    up = [(i, (i + 1) % count) for i in range(count)]
    down = [(j, i) for i, j in up]
    last = lax.slice_in_dim(x, length - width, length, axis=dim)
    first = lax.slice_in_dim(x, 0, width, axis=dim)
    return lax.ppermute(last, axis, up), lax.ppermute(first, axis, down)


def widen(x, axis, dim):
    before, after = shifted(x, axis, dim, 1)
    return jnp.concatenate([before, x, after], axis=dim)


def message_kernel(cells_y, cells_z, fold_z, levels, home_ref, feat_ref, geom_ref, wb_ref, out_ref, hb, phi, acc):
    cell = pl.program_id(0)
    x = cell // (cells_y * cells_z)
    y = (cell // cells_z) % cells_y
    z = cell % cells_z
    slots = out_ref.shape[1]
    feat = out_ref.shape[2]
    near_z = feat_ref.shape[3]
    chunk = 32
    for a in range(3):
        hb[a] = jnp.broadcast_to(home_ref[0, :, a : a + 1], (slots, slots))
    for ox in range(3):
        for oy in range(3):
            for oz in range(near_z):
                g = geom_ref[x + ox, z, y + oy, oz]
                nx = g[0:1] + (ox - 1.0)
                ny = g[1:2] + (oy - 1.0)
                if fold_z:
                    nz = g[2:3]
                else:
                    nz = g[2:3] + (oz - 1.0)
                col = (oy * near_z + oz) * slots
                center = ox == 1 and oy == 1 and oz == (0 if fold_z else 1)
                for p0 in range(0, slots, chunk):
                    dx = nx - hb[0, p0 : p0 + chunk]
                    dy = ny - hb[1, p0 : p0 + chunk]
                    dz = nz - hb[2, p0 : p0 + chunk]
                    if fold_z and oz == 1:
                        dz = 1.0 - jnp.abs(dz)
                    radial_terms(dx, dy, dz, levels, center, p0, phi.at[ox], col, slots)
        rows = feat_ref[x + ox, z, pl.ds(y, 3)].reshape(3 * near_z * slots, feat)
        part = jnp.dot(phi[ox], rows, preferred_element_type=jnp.float32)
        if ox == 0:
            acc[...] = part
        elif ox == 1:
            acc[...] += part
    total = jnp.zeros((slots, feat), jnp.float32)
    for b in range(levels):
        both = acc[b * slots : (b + 1) * slots] + part[b * slots : (b + 1) * slots]
        total = total + both * wb_ref[b : b + 1]
    out_ref[0] = total.astype(jnp.bfloat16)


def basis_kernel(pos_ref, wave_ref, feat_ref, basis_ref, struct_ref):
    cell = pl.program_id(0)
    waves = wave_ref.shape[0]
    pos = pos_ref[0]
    chunk = 64
    for w0 in range(0, waves, chunk):
        wv = wave_ref[w0 : w0 + chunk]
        turns = wv[:, 0:1] * pos[0:1] + wv[:, 1:2] * pos[1:2] + wv[:, 2:3] * pos[2:3]
        u = turns - jnp.floor(turns + 0.5)
        q = u * u
        s = u * poly(q, SIN_C)
        c = poly(q, COS_C)
        basis_ref[0, w0 : w0 + chunk] = (1.0 - 2.0 * s * s).astype(jnp.bfloat16)
        basis_ref[0, waves + w0 : waves + w0 + chunk] = (2.0 * s * c).astype(jnp.bfloat16)
    part = jnp.dot(basis_ref[0], feat_ref[0], preferred_element_type=jnp.float32)

    @pl.when(cell == 0)
    def _():
        struct_ref[...] = part

    @pl.when(cell > 0)
    def _():
        struct_ref[...] += part


def final_kernel(basis_ref, grid_ref, msg_ref, feat_ref, home_ref, wm_ref, wo_ref, out_ref):
    far = lax.dot_general(
        basis_ref[0], grid_ref[...], (((0,), (0,)), ((), ())), preferred_element_type=jnp.float32
    )
    joined = far + jnp.dot(msg_ref[0], wm_ref[...], preferred_element_type=jnp.float32)
    hidden = (joined / (1.0 + jnp.exp(-joined))).astype(jnp.bfloat16)
    result = feat_ref[0].astype(jnp.float32) + jnp.dot(hidden, wo_ref[...], preferred_element_type=jnp.float32)
    out_ref[0] = (result * home_ref[0, :, 3:4]).astype(jnp.bfloat16)


def coords(index, counts):
    return (index // (counts[1] * counts[2]), (index // counts[2]) % counts[1], index % counts[2])


def layer_kernel(
    counts,
    levels,
    pack_ref,
    home_ref,
    pos_ref,
    wave_ref,
    wb_ref,
    damp_ref,
    mix_ref,
    we_ref,
    wm_ref,
    wo_ref,
    out_ref,
    wide,
    hb,
    phi,
    acc,
    basis,
    struct,
    pair,
    chip_sum,
    parts,
    share,
    field,
    msg,
    halo_send,
    halo_recv,
    side_send,
    side_recv,
    own_sem,
    pair_send,
    pair_recv,
    part_send,
    part_recv,
    share_send,
    share_recv,
):
    cx, cy = pack_ref.shape[0], pack_ref.shape[1]
    cells, slots, feat = out_ref.shape
    waves = wave_ref.shape[0]
    devices = counts[0] * counts[1] * counts[2]
    rows = waves // devices
    at = (lax.axis_index("gx"), lax.axis_index("gy"), lax.axis_index("gz"))
    chips = counts[0] * counts[1]
    chip = at[0] * counts[1] + at[1]
    core = at[2]
    mesh_id = pl.DeviceIdType.MESH

    partner = (at[0], at[1], 1 - core)

    def same_core(k):
        peer = (chip + k) % chips
        return (peer // counts[1], peer % counts[1], core)

    def to_partner(src, dst, send, recv):
        return pltpu.make_async_remote_copy(
            src_ref=src, dst_ref=dst, send_sem=send, recv_sem=recv, device_id=partner, device_id_type=mesh_id
        )

    barrier = pltpu.get_barrier_semaphore()

    @pl.loop(1, chips)
    def _(k):
        pl.semaphore_signal(barrier, inc=1, device_id=same_core(k), device_id_type=mesh_id)

    pl.semaphore_signal(barrier, inc=1, device_id=partner, device_id_type=mesh_id)
    pl.semaphore_wait(barrier, chips)

    own = pltpu.make_async_copy(pack_ref, wide.at[pl.ds(1, cx), pl.ds(1, cy), 0], own_sem)
    own.start()

    def span(step, length):
        if step == 0:
            return 0, 1, length
        if step == 1:
            return length - 1, 0, 1
        return 0, length + 1, 1

    halo, side = [], []
    for dx in (1, -1, 0):
        for dy in (1, -1, 0):
            n = len(halo)
            sx, tx, lx = span(dx, cx)
            sy, ty, ly = span(dy, cy)
            region = (pl.ds(tx, lx), pl.ds(ty, ly))
            if (dx, dy) == (0, 0):
                side.append(to_partner(pack_ref, wide.at[(*region, 1)], side_send.at[n], side_recv.at[n]))
                continue
            target = ((at[0] + dx + counts[0]) % counts[0], (at[1] + dy + counts[1]) % counts[1], core)
            copy = pltpu.make_async_remote_copy(
                src_ref=pack_ref.at[pl.ds(sx, lx), pl.ds(sy, ly)],
                dst_ref=wide.at[(*region, 0)],
                send_sem=halo_send.at[n],
                recv_sem=halo_recv.at[n],
                device_id=target,
                device_id_type=mesh_id,
            )
            copy.start()
            halo.append(copy)
            side.append(to_partner(wide.at[(*region, 0)], wide.at[(*region, 1)], side_send.at[n], side_recv.at[n]))
    side[-1].start()

    @pl.loop(0, cells)
    def _(cell):
        pos = pos_ref[cell]
        lanes = pl.ds(pl.multiple_of(cell * slots, slots), slots)
        chunk = 64
        for w0 in range(0, waves, chunk):
            wv = wave_ref[w0 : w0 + chunk]
            turns = wv[:, 0:1] * pos[0:1] + wv[:, 1:2] * pos[1:2] + wv[:, 2:3] * pos[2:3]
            u = turns - jnp.floor(turns + 0.5)
            q = u * u
            s = u * poly(q, SIN_C)
            c = poly(q, COS_C)
            basis[w0 : w0 + chunk, lanes] = (1.0 - 2.0 * s * s).astype(jnp.bfloat16)
            basis[waves + w0 : waves + w0 + chunk, lanes] = (2.0 * s * c).astype(jnp.bfloat16)

    atoms = pack_ref[:, :, 0:slots, :].reshape(cells * slots, feat)
    struct[...] = (
        jnp.dot(basis[...], atoms, preferred_element_type=jnp.float32)
        .astype(jnp.bfloat16)
        .reshape(2, chips, 2, rows, feat)
    )
    swap = to_partner(struct.at[:, :, 1 - core], pair, pair_send.at[0], pair_recv.at[0])
    swap.start()

    def part_copy(k):
        return pltpu.make_async_remote_copy(
            src_ref=chip_sum.at[:, (chip + k) % chips],
            dst_ref=parts.at[k],
            send_sem=part_send.at[k],
            recv_sem=part_recv.at[k],
            device_id=same_core(k),
            device_id_type=mesh_id,
        )

    def share_copy(k, slot):
        return pltpu.make_async_remote_copy(
            src_ref=share,
            dst_ref=field.at[:, slot, core],
            send_sem=share_send.at[k],
            recv_sem=share_recv.at[k],
            device_id=same_core(k),
            device_id_type=mesh_id,
        )

    def field_copy(half):
        mine = field.at[:, :, half]
        return to_partner(mine, mine, pair_send.at[1], pair_recv.at[1])

    swap.wait()
    both = struct[:, :, core].astype(jnp.float32) + pair[...].astype(jnp.float32)
    chip_sum[...] = both.astype(jnp.bfloat16)

    @pl.loop(1, chips)
    def _(k):
        part_copy(k).start()

    own.wait()
    for n, copy in enumerate(halo):
        copy.wait()
        side[n].start()
    for copy in side:
        copy.wait()

    @pl.loop(0, cells)
    def _(cell):
        @pl.when(cell == cells // 4)
        def _():
            @pl.loop(1, chips)
            def _(k):
                part_copy(k).wait()

            parts[0] = chip_sum[:, chip]
            total = jnp.sum(parts[...].astype(jnp.float32), axis=0).reshape(2 * rows, feat)
            mixed = jnp.dot(total, mix_ref[...], precision=lax.Precision.HIGHEST, preferred_element_type=jnp.float32)
            filtered = (mixed * damp_ref[...]).astype(jnp.bfloat16)
            projected = jnp.dot(filtered, we_ref[...], preferred_element_type=jnp.float32)
            projected = projected.astype(jnp.bfloat16).reshape(2, rows, feat)
            share[...] = projected
            field[:, chip, core] = projected

            @pl.loop(1, chips)
            def _(k):
                share_copy(k, chip).start()

        @pl.when(cell == cells - 1)
        def _():
            @pl.loop(1, chips)
            def _(k):
                share_copy(k, (chip - k + chips) % chips).wait()

            field_copy(core).start()

        x = cell // cy
        y = cell % cy
        for a in range(3):
            hb[a] = jnp.broadcast_to(home_ref[cell, :, a : a + 1], (slots, slots))
        chunk = 32
        for ox in range(3):
            for oy in range(3):
                for oz in range(2):
                    g = wide[x + ox, y + oy, oz, slots : slots + 16, 0:slots].astype(jnp.float32)
                    nx = g[0:1] + (ox - 1.0)
                    ny = g[1:2] + (oy - 1.0)
                    nz = g[2:3]
                    col = (oy * 2 + oz) * slots
                    for p0 in range(0, slots, chunk):
                        gx = nx - hb[0, p0 : p0 + chunk]
                        gy = ny - hb[1, p0 : p0 + chunk]
                        gz = nz - hb[2, p0 : p0 + chunk]
                        if oz == 1:
                            gz = 1.0 - jnp.abs(gz)
                        radial_terms(gx, gy, gz, levels, (ox, oy, oz) == (1, 1, 0), p0, phi.at[ox], col, slots)
            near = wide[x + ox, pl.ds(y, 3), :, 0:slots].reshape(6 * slots, feat)
            part = jnp.dot(phi[ox], near, preferred_element_type=jnp.float32)
            if ox == 0:
                acc[...] = part
            elif ox == 1:
                acc[...] += part
        total = jnp.zeros((slots, feat), jnp.float32)
        for b in range(levels):
            both = acc[b * slots : (b + 1) * slots] + part[b * slots : (b + 1) * slots]
            total = total + both * wb_ref[b : b + 1]
        msg[cell] = total.astype(jnp.bfloat16)

    field_copy(core).wait_send()
    field_copy(1 - core).wait_recv()

    waves_field = field[...].reshape(2 * waves, feat)

    @pl.loop(0, cells)
    def _(cell):
        lanes = pl.ds(pl.multiple_of(cell * slots, slots), slots)
        far = lax.dot_general(
            basis[:, lanes], waves_field, (((0,), (0,)), ((), ())), preferred_element_type=jnp.float32
        )
        joined = far + jnp.dot(msg[cell], wm_ref[...], preferred_element_type=jnp.float32)
        hidden = (joined / (1.0 + jnp.exp(-joined))).astype(jnp.bfloat16)
        atom = pack_ref[cell // cy, cell % cy, 0:slots].astype(jnp.float32)
        result = atom + jnp.dot(hidden, wo_ref[...], preferred_element_type=jnp.float32)
        out_ref[cell] = (result * home_ref[cell, :, 3:4]).astype(jnp.bfloat16)


def radial_terms(gx, gy, gz, levels, center, p0, phi, col, slots):
    rows = gx.shape[0]
    sq = jnp.minimum(gx * gx + gy * gy + gz * gz, 1.0)
    dist = sq * lax.rsqrt(jnp.maximum(sq, 1e-30))
    ratio = jnp.exp2(dist * (2.0 * sharpness / (levels - 1) * math.log2(math.e)))
    edge = 1.0 - sq
    val = edge * edge * jnp.exp2(sq * (-sharpness * math.log2(math.e)))
    if center:
        row = lax.broadcasted_iota(jnp.int32, val.shape, 0) + p0
        lane = lax.broadcasted_iota(jnp.int32, val.shape, 1)
        val = jnp.where(row == lane, 0.0, val)
    for b in range(levels):
        phi[b * slots + p0 : b * slots + p0 + rows, col : col + slots] = val.astype(jnp.bfloat16)
        if b + 1 < levels:
            val = val * ratio


def body(
    features,
    fractions,
    occupied,
    wave_index,
    radial_weight,
    ewald_mix,
    msg_weight,
    ewald_weight,
    out_weight,
):
    cx, cy, cz, slots, feat = features.shape
    levels, heads = radial_weight.shape
    cells = cx * cy * cz
    grid = [lax.axis_size("gx") * cx, lax.axis_size("gy") * cy, lax.axis_size("gz") * cz]
    devices = lax.axis_size("gx") * lax.axis_size("gy") * lax.axis_size("gz")
    waves = wave_index.shape[1]
    axes = ("gx", "gy", "gz")
    full = lambda shape: pl.BlockSpec(shape, lambda i: (0,) * len(shape))
    params = pltpu.CompilerParams(dimension_semantics=("arbitrary",), vmem_limit_bytes=56 * 2**20)

    masked = features * occupied[..., None].astype(jnp.bfloat16)
    frac = fractions.astype(jnp.float32)
    cell_feat = masked.reshape(cells, slots, feat)
    home = jnp.concatenate([frac, occupied[:, :, :, None, :].astype(jnp.float32)], axis=3)
    home = jnp.swapaxes(home.reshape(cells, 4, slots), 1, 2)

    start = [
        (lax.axis_index(n) * c + jnp.arange(c, dtype=jnp.int32)).astype(jnp.float32)
        for n, c in zip(axes, (cx, cy, cz))
    ]
    origin = jnp.stack(jnp.meshgrid(*start, indexing="ij"), axis=-1)[..., None]
    pos = (origin + frac).reshape(cells, 3, slots)
    lengths = jnp.array(grid, jnp.float32)
    index = wave_index.astype(jnp.float32)
    wave_vec = 2.0 * math.pi * index / lengths[:, None]
    wave_sq = jnp.sum(wave_vec * wave_vec, axis=0)
    damping = (
        strength
        * jnp.exp(-0.5 * smearing * wave_sq)
        / (wave_sq + screening)
        * (1.0 / math.sqrt(cells * slots * devices * waves))
    )
    wave_turn = (index / lengths[:, None]).T

    fold_z = grid[2] == 2 and cz == 1
    level = jnp.arange(levels, dtype=jnp.float32) / (levels - 1)
    wb = radial_weight * (jnp.exp(-sharpness * level * level) / math.sqrt(4.0 * slots))[:, None]
    wb = jnp.repeat(wb, feat // heads, axis=1)
    counts = tuple(lax.axis_size(n) for n in axes)
    rows = waves // devices
    chips = counts[0] * counts[1]
    if fold_z and rows % 16 == 0 and min(counts) > 1:
        spread = jnp.pad(fractions, ((0, 0),) * 3 + ((0, 13), (0, feat - slots)))
        pack = jnp.concatenate([masked, spread], axis=3).reshape(cx, cy, slots + 16, feat)
        damp = lax.dynamic_slice_in_dim(damping, lax.axis_index(axes) * rows, rows, 0)
        damp = jnp.concatenate([damp, damp]).reshape(2 * rows, 1)
        vmem = pl.BlockSpec(memory_space=pltpu.VMEM)
        dma = pltpu.SemaphoreType.DMA
        out = pl.pallas_call(
            functools.partial(layer_kernel, counts, levels),
            in_specs=[vmem] * 10,
            out_specs=vmem,
            out_shape=jax.ShapeDtypeStruct((cells, slots, feat), jnp.bfloat16),
            scratch_shapes=[
                pltpu.VMEM((cx + 2, cy + 2, 2, slots + 16, feat), jnp.bfloat16),
                pltpu.VMEM((3, slots, slots), jnp.float32),
                pltpu.VMEM((3, levels * slots, 6 * slots), jnp.bfloat16),
                pltpu.VMEM((levels * slots, feat), jnp.float32),
                pltpu.VMEM((2 * waves, cells * slots), jnp.bfloat16),
                pltpu.VMEM((2, chips, 2, rows, feat), jnp.bfloat16),
                pltpu.VMEM((2, chips, rows, feat), jnp.bfloat16),
                pltpu.VMEM((2, chips, rows, feat), jnp.bfloat16),
                pltpu.VMEM((chips, 2, rows, feat), jnp.bfloat16),
                pltpu.VMEM((2, rows, feat), jnp.bfloat16),
                pltpu.VMEM((2, chips, 2, rows, feat), jnp.bfloat16),
                pltpu.VMEM((cells, slots, feat), jnp.bfloat16),
                dma((8,)),
                dma((8,)),
                dma((9,)),
                dma((9,)),
                dma,
                dma((2,)),
                dma((2,)),
                dma((chips,)),
                dma((chips,)),
                dma((chips,)),
                dma((chips,)),
            ],
            compiler_params=pltpu.CompilerParams(
                collective_id=0, has_side_effects=True, vmem_limit_bytes=56 * 2**20
            ),
            name="layer",
        )(pack, home, pos, wave_turn, wb, damp, ewald_mix, ewald_weight, msg_weight, out_weight)
        return out.reshape(features.shape)

    basis, struct = pl.pallas_call(
        basis_kernel,
        grid=(cells,),
        in_specs=[
            pl.BlockSpec((1, 3, slots), lambda i: (i, 0, 0)),
            full((waves, 3)),
            pl.BlockSpec((1, slots, feat), lambda i: (i, 0, 0)),
        ],
        out_specs=[pl.BlockSpec((1, 2 * waves, slots), lambda i: (i, 0, 0)), full((2 * waves, feat))],
        out_shape=[
            jax.ShapeDtypeStruct((cells, 2 * waves, slots), jnp.bfloat16),
            jax.ShapeDtypeStruct((2 * waves, feat), jnp.float32),
        ],
        compiler_params=params,
        name="basis",
    )(pos, wave_turn, cell_feat)

    wave_share = lax.psum_scatter(struct.reshape(2, waves, feat), axes, scatter_dimension=1, tiled=True)
    share_rows = wave_share.shape[1]
    share_damp = lax.dynamic_slice_in_dim(damping, lax.axis_index(axes) * share_rows, share_rows, 0)
    mixed = jnp.dot(wave_share.reshape(2 * share_rows, feat), ewald_mix, precision=lax.Precision.HIGHEST)
    filtered = (mixed.reshape(2, share_rows, feat) * share_damp[None, :, None]).astype(jnp.bfloat16)
    projected = jnp.dot(filtered, ewald_weight, preferred_element_type=jnp.float32).astype(jnp.bfloat16)
    field = lax.all_gather(projected, axes, axis=1, tiled=True).reshape(2 * waves, feat)

    wide_feat = widen(widen(masked, "gx", 0), "gy", 1)
    wide_geom = widen(widen(fractions, "gx", 0), "gy", 1)
    if fold_z:
        swap = [(0, 1), (1, 0)]
        wide_feat = jnp.concatenate([wide_feat, lax.ppermute(wide_feat, "gz", swap)], axis=2)
        wide_geom = jnp.concatenate([wide_geom, lax.ppermute(wide_geom, "gz", swap)], axis=2)
        near_z = 2
    else:
        wide_feat = widen(wide_feat, "gz", 2)
        wide_geom = widen(wide_geom, "gz", 2)
        near_z = 3
    wide_feat = jnp.stack([wide_feat[:, :, z : z + near_z] for z in range(cz)], axis=1)
    wide_geom = jnp.stack([wide_geom[:, :, z : z + near_z] for z in range(cz)], axis=1).astype(jnp.float32)
    messages = pl.pallas_call(
        functools.partial(message_kernel, cy, cz, fold_z, levels),
        grid=(cells,),
        in_specs=[
            pl.BlockSpec((1, slots, 4), lambda i: (i, 0, 0)),
            full(wide_feat.shape),
            full(wide_geom.shape),
            full(wb.shape),
        ],
        out_specs=pl.BlockSpec((1, slots, feat), lambda i: (i, 0, 0)),
        out_shape=jax.ShapeDtypeStruct((cells, slots, feat), jnp.bfloat16),
        scratch_shapes=[
            pltpu.VMEM((3, slots, slots), jnp.float32),
            pltpu.VMEM((3, levels * slots, 3 * near_z * slots), jnp.bfloat16),
            pltpu.VMEM((levels * slots, feat), jnp.float32),
        ],
        compiler_params=params,
        cost_estimate=pl.CostEstimate(
            flops=2 * cells * levels * slots * 9 * near_z * slots * feat, bytes_accessed=2**22, transcendentals=0
        ),
        name="messages",
    )(home, wide_feat, wide_geom, wb)

    out = pl.pallas_call(
        final_kernel,
        grid=(cells,),
        in_specs=[
            pl.BlockSpec((1, 2 * waves, slots), lambda i: (i, 0, 0)),
            full((2 * waves, feat)),
            pl.BlockSpec((1, slots, feat), lambda i: (i, 0, 0)),
            pl.BlockSpec((1, slots, feat), lambda i: (i, 0, 0)),
            pl.BlockSpec((1, slots, 4), lambda i: (i, 0, 0)),
            full((feat, feat)),
            full((feat, feat)),
        ],
        out_specs=pl.BlockSpec((1, slots, feat), lambda i: (i, 0, 0)),
        out_shape=jax.ShapeDtypeStruct((cells, slots, feat), jnp.bfloat16),
        compiler_params=params,
        name="final",
    )(basis, field, messages, cell_feat, home, msg_weight, out_weight)
    return out.reshape(features.shape)


def solution(mesh):
    cell = P("gx", "gy", "gz", None, None)
    in_specs = (cell, cell, P("gx", "gy", "gz", None), P(), P(), P(), P(), P(), P())
    return jax.shard_map(body, mesh=mesh, in_specs=in_specs, out_specs=cell, check_vma=False)
```

```python
import functools
import math

import jax
import jax.numpy as jnp
from jax import lax
from jax.experimental import pallas as pl
from jax.experimental.pallas import tpu as pltpu
from jax.sharding import PartitionSpec as P

sharpness = 16.0
smearing = 0.04
screening = 4.0
strength = 24.0

SIN_C = [(-1.0) ** k * math.pi ** (2 * k + 1) / math.factorial(2 * k + 1) for k in range(7)]
COS_C = [(-1.0) ** k * math.pi ** (2 * k) / math.factorial(2 * k) for k in range(7)]


def poly(z, coefs):
    acc = jnp.full_like(z, coefs[-1])
    for c in coefs[-2::-1]:
        acc = acc * z + c
    return acc


def shifted(x, axis, dim, width):
    count, length = lax.axis_size(axis), x.shape[dim]
    up = [(i, (i + 1) % count) for i in range(count)]
    down = [(j, i) for i, j in up]
    last = lax.slice_in_dim(x, length - width, length, axis=dim)
    first = lax.slice_in_dim(x, 0, width, axis=dim)
    return lax.ppermute(last, axis, up), lax.ppermute(first, axis, down)


def widen(x, axis, dim):
    before, after = shifted(x, axis, dim, 1)
    return jnp.concatenate([before, x, after], axis=dim)


def message_kernel(cells_y, cells_z, fold_z, levels, home_ref, feat_ref, geom_ref, wb_ref, out_ref, hb, phi, acc):
    cell = pl.program_id(0)
    x = cell // (cells_y * cells_z)
    y = (cell // cells_z) % cells_y
    z = cell % cells_z
    slots = out_ref.shape[1]
    feat = out_ref.shape[2]
    near_z = feat_ref.shape[3]
    chunk = 32
    for a in range(3):
        hb[a] = jnp.broadcast_to(home_ref[0, :, a : a + 1], (slots, slots))
    for ox in range(3):
        for oy in range(3):
            for oz in range(near_z):
                g = geom_ref[x + ox, z, y + oy, oz]
                nx = g[0:1] + (ox - 1.0)
                ny = g[1:2] + (oy - 1.0)
                if fold_z:
                    nz = g[2:3]
                else:
                    nz = g[2:3] + (oz - 1.0)
                col = (oy * near_z + oz) * slots
                center = ox == 1 and oy == 1 and oz == (0 if fold_z else 1)
                for p0 in range(0, slots, chunk):
                    dx = nx - hb[0, p0 : p0 + chunk]
                    dy = ny - hb[1, p0 : p0 + chunk]
                    dz = nz - hb[2, p0 : p0 + chunk]
                    if fold_z and oz == 1:
                        dz = 1.0 - jnp.abs(dz)
                    radial_terms(dx, dy, dz, levels, center, p0, phi.at[ox], col, slots)
        rows = feat_ref[x + ox, z, pl.ds(y, 3)].reshape(3 * near_z * slots, feat)
        part = jnp.dot(phi[ox], rows, preferred_element_type=jnp.float32)
        if ox == 0:
            acc[...] = part
        elif ox == 1:
            acc[...] += part
    total = jnp.zeros((slots, feat), jnp.float32)
    for b in range(levels):
        both = acc[b * slots : (b + 1) * slots] + part[b * slots : (b + 1) * slots]
        total = total + both * wb_ref[b : b + 1]
    out_ref[0] = total.astype(jnp.bfloat16)


def basis_kernel(pos_ref, wave_ref, feat_ref, basis_ref, struct_ref):
    cell = pl.program_id(0)
    waves = wave_ref.shape[0]
    pos = pos_ref[0]
    chunk = 64
    for w0 in range(0, waves, chunk):
        wv = wave_ref[w0 : w0 + chunk]
        turns = wv[:, 0:1] * pos[0:1] + wv[:, 1:2] * pos[1:2] + wv[:, 2:3] * pos[2:3]
        u = turns - jnp.floor(turns + 0.5)
        q = u * u
        s = u * poly(q, SIN_C)
        c = poly(q, COS_C)
        basis_ref[0, w0 : w0 + chunk] = (1.0 - 2.0 * s * s).astype(jnp.bfloat16)
        basis_ref[0, waves + w0 : waves + w0 + chunk] = (2.0 * s * c).astype(jnp.bfloat16)
    part = jnp.dot(basis_ref[0], feat_ref[0], preferred_element_type=jnp.float32)

    @pl.when(cell == 0)
    def _():
        struct_ref[...] = part

    @pl.when(cell > 0)
    def _():
        struct_ref[...] += part


def final_kernel(basis_ref, grid_ref, msg_ref, feat_ref, home_ref, wm_ref, wo_ref, out_ref):
    far = lax.dot_general(
        basis_ref[0], grid_ref[...], (((0,), (0,)), ((), ())), preferred_element_type=jnp.float32
    )
    joined = far + jnp.dot(msg_ref[0], wm_ref[...], preferred_element_type=jnp.float32)
    hidden = (joined / (1.0 + jnp.exp(-joined))).astype(jnp.bfloat16)
    result = feat_ref[0].astype(jnp.float32) + jnp.dot(hidden, wo_ref[...], preferred_element_type=jnp.float32)
    out_ref[0] = (result * home_ref[0, :, 3:4]).astype(jnp.bfloat16)


def coords(index, counts):
    return (index // (counts[1] * counts[2]), (index // counts[2]) % counts[1], index % counts[2])


def layer_kernel(
    counts,
    levels,
    pack_ref,
    home_ref,
    pos_ref,
    wave_ref,
    wb_ref,
    damp_ref,
    mix_ref,
    we_ref,
    wm_ref,
    wo_ref,
    out_ref,
    wide,
    hb,
    phi,
    acc,
    basis,
    struct,
    pair,
    chip_sum,
    parts,
    share,
    field,
    msg,
    halo_send,
    halo_recv,
    side_send,
    side_recv,
    own_sem,
    pair_send,
    pair_recv,
    part_send,
    part_recv,
    share_send,
    share_recv,
):
    cx, cy = pack_ref.shape[0], pack_ref.shape[1]
    cells, slots, feat = out_ref.shape
    waves = wave_ref.shape[0]
    devices = counts[0] * counts[1] * counts[2]
    rows = waves // devices
    at = (lax.axis_index("gx"), lax.axis_index("gy"), lax.axis_index("gz"))
    chips = counts[0] * counts[1]
    chip = at[0] * counts[1] + at[1]
    core = at[2]
    mesh_id = pl.DeviceIdType.MESH

    partner = (at[0], at[1], 1 - core)

    def same_core(k):
        peer = (chip + k) % chips
        return (peer // counts[1], peer % counts[1], core)

    def to_partner(src, dst, send, recv):
        return pltpu.make_async_remote_copy(
            src_ref=src, dst_ref=dst, send_sem=send, recv_sem=recv, device_id=partner, device_id_type=mesh_id
        )

    barrier = pltpu.get_barrier_semaphore()

    @pl.loop(1, chips)
    def _(k):
        pl.semaphore_signal(barrier, inc=1, device_id=same_core(k), device_id_type=mesh_id)

    pl.semaphore_signal(barrier, inc=1, device_id=partner, device_id_type=mesh_id)
    pl.semaphore_wait(barrier, chips)

    own = pltpu.make_async_copy(pack_ref, wide.at[pl.ds(1, cx), pl.ds(1, cy), 0], own_sem)
    own.start()

    def span(step, length):
        if step == 0:
            return 0, 1, length
        if step == 1:
            return length - 1, 0, 1
        return 0, length + 1, 1

    halo, side = [], []
    for dx in (1, -1, 0):
        for dy in (1, -1, 0):
            n = len(halo)
            sx, tx, lx = span(dx, cx)
            sy, ty, ly = span(dy, cy)
            region = (pl.ds(tx, lx), pl.ds(ty, ly))
            if (dx, dy) == (0, 0):
                side.append(to_partner(pack_ref, wide.at[(*region, 1)], side_send.at[n], side_recv.at[n]))
                continue
            target = ((at[0] + dx + counts[0]) % counts[0], (at[1] + dy + counts[1]) % counts[1], core)
            copy = pltpu.make_async_remote_copy(
                src_ref=pack_ref.at[pl.ds(sx, lx), pl.ds(sy, ly)],
                dst_ref=wide.at[(*region, 0)],
                send_sem=halo_send.at[n],
                recv_sem=halo_recv.at[n],
                device_id=target,
                device_id_type=mesh_id,
            )
            copy.start()
            halo.append(copy)
            side.append(to_partner(wide.at[(*region, 0)], wide.at[(*region, 1)], side_send.at[n], side_recv.at[n]))
    side[-1].start()

    @pl.loop(0, cells)
    def _(cell):
        pos = pos_ref[cell]
        filled = pack_ref[cell // cy, cell % cy, slots : slots + 16, 0:slots].astype(jnp.float32)[3:4]
        lanes = pl.ds(pl.multiple_of(cell * slots, slots), slots)
        chunk = 64
        for w0 in range(0, waves, chunk):
            wv = wave_ref[w0 : w0 + chunk]
            turns = wv[:, 0:1] * pos[0:1] + wv[:, 1:2] * pos[1:2] + wv[:, 2:3] * pos[2:3]
            u = turns - jnp.floor(turns + 0.5)
            q = u * u
            s = u * poly(q, SIN_C)
            c = poly(q, COS_C)
            basis[w0 : w0 + chunk, lanes] = (filled * (1.0 - 2.0 * s * s)).astype(jnp.bfloat16)
            basis[waves + w0 : waves + w0 + chunk, lanes] = (filled * (2.0 * s * c)).astype(jnp.bfloat16)

    atoms = pack_ref[:, :, 0:slots, :].reshape(cells * slots, feat)
    struct[...] = (
        jnp.dot(basis[...], atoms, preferred_element_type=jnp.float32)
        .astype(jnp.bfloat16)
        .reshape(2, chips, 2, rows, feat)
    )
    swap = to_partner(struct.at[:, :, 1 - core], pair, pair_send.at[0], pair_recv.at[0])
    swap.start()

    def part_copy(k):
        return pltpu.make_async_remote_copy(
            src_ref=chip_sum.at[:, (chip + k) % chips],
            dst_ref=parts.at[k],
            send_sem=part_send.at[k],
            recv_sem=part_recv.at[k],
            device_id=same_core(k),
            device_id_type=mesh_id,
        )

    def share_copy(k, slot):
        return pltpu.make_async_remote_copy(
            src_ref=share,
            dst_ref=field.at[:, slot, core],
            send_sem=share_send.at[k],
            recv_sem=share_recv.at[k],
            device_id=same_core(k),
            device_id_type=mesh_id,
        )

    def field_copy(half):
        mine = field.at[:, :, half]
        return to_partner(mine, mine, pair_send.at[1], pair_recv.at[1])

    swap.wait()
    both = struct[:, :, core].astype(jnp.float32) + pair[...].astype(jnp.float32)
    chip_sum[...] = both.astype(jnp.bfloat16)

    @pl.loop(1, chips)
    def _(k):
        part_copy(k).start()

    own.wait()
    for n, copy in enumerate(halo):
        copy.wait()
        side[n].start()
    for copy in side:
        copy.wait()

    @pl.loop(0, cells)
    def _(cell):
        @pl.when(cell == cells // 4)
        def _():
            @pl.loop(1, chips)
            def _(k):
                part_copy(k).wait()

            parts[0] = chip_sum[:, chip]
            total = jnp.sum(parts[...].astype(jnp.float32), axis=0).reshape(2 * rows, feat)
            mixed = jnp.dot(total, mix_ref[...], precision=lax.Precision.HIGHEST, preferred_element_type=jnp.float32)
            filtered = (mixed * damp_ref[...]).astype(jnp.bfloat16)
            projected = jnp.dot(filtered, we_ref[...], preferred_element_type=jnp.float32)
            projected = projected.astype(jnp.bfloat16).reshape(2, rows, feat)
            share[...] = projected
            field[:, chip, core] = projected

            @pl.loop(1, chips)
            def _(k):
                share_copy(k, chip).start()

        @pl.when(cell == cells - 1)
        def _():
            @pl.loop(1, chips)
            def _(k):
                share_copy(k, (chip - k + chips) % chips).wait()

            field_copy(core).start()

        x = cell // cy
        y = cell % cy
        for a in range(3):
            hb[a] = jnp.broadcast_to(home_ref[cell, :, a : a + 1], (slots, slots))
        chunk = 32
        for ox in range(3):
            for oy in range(3):
                for oz in range(2):
                    g = wide[x + ox, y + oy, oz, slots : slots + 16, 0:slots].astype(jnp.float32)
                    nx = g[0:1] + (ox - 1.0)
                    ny = g[1:2] + (oy - 1.0)
                    nz = g[2:3]
                    col = (oy * 2 + oz) * slots
                    for p0 in range(0, slots, chunk):
                        gx = nx - hb[0, p0 : p0 + chunk]
                        gy = ny - hb[1, p0 : p0 + chunk]
                        gz = nz - hb[2, p0 : p0 + chunk]
                        if oz == 1:
                            gz = 1.0 - jnp.abs(gz)
                        radial_terms(gx, gy, gz, levels, (ox, oy, oz) == (1, 1, 0), p0, phi.at[ox], col, slots, g[3:4])
            near = wide[x + ox, pl.ds(y, 3), :, 0:slots].reshape(6 * slots, feat)
            part = jnp.dot(phi[ox], near, preferred_element_type=jnp.float32)
            if ox == 0:
                acc[...] = part
            elif ox == 1:
                acc[...] += part
        total = jnp.zeros((slots, feat), jnp.float32)
        for b in range(levels):
            both = acc[b * slots : (b + 1) * slots] + part[b * slots : (b + 1) * slots]
            total = total + both * wb_ref[b : b + 1]
        msg[cell] = total.astype(jnp.bfloat16)

    field_copy(core).wait_send()
    field_copy(1 - core).wait_recv()

    waves_field = field[...].reshape(2 * waves, feat)

    @pl.loop(0, cells)
    def _(cell):
        lanes = pl.ds(pl.multiple_of(cell * slots, slots), slots)
        far = lax.dot_general(
            basis[:, lanes], waves_field, (((0,), (0,)), ((), ())), preferred_element_type=jnp.float32
        )
        joined = far + jnp.dot(msg[cell], wm_ref[...], preferred_element_type=jnp.float32)
        hidden = (joined / (1.0 + jnp.exp(-joined))).astype(jnp.bfloat16)
        atom = pack_ref[cell // cy, cell % cy, 0:slots].astype(jnp.float32)
        result = atom + jnp.dot(hidden, wo_ref[...], preferred_element_type=jnp.float32)
        out_ref[cell] = (result * home_ref[cell, :, 3:4]).astype(jnp.bfloat16)


def radial_terms(gx, gy, gz, levels, center, p0, phi, col, slots, filled=None):
    rows = gx.shape[0]
    sq = jnp.minimum(gx * gx + gy * gy + gz * gz, 1.0)
    dist = sq * lax.rsqrt(jnp.maximum(sq, 1e-30))
    ratio = jnp.exp2(dist * (2.0 * sharpness / (levels - 1) * math.log2(math.e)))
    edge = 1.0 - sq
    val = edge * edge * jnp.exp2(sq * (-sharpness * math.log2(math.e)))
    if filled is not None:
        val = val * filled
    if center:
        row = lax.broadcasted_iota(jnp.int32, val.shape, 0) + p0
        lane = lax.broadcasted_iota(jnp.int32, val.shape, 1)
        val = jnp.where(row == lane, 0.0, val)
    for b in range(levels):
        phi[b * slots + p0 : b * slots + p0 + rows, col : col + slots] = val.astype(jnp.bfloat16)
        if b + 1 < levels:
            val = val * ratio


def body(
    features,
    fractions,
    occupied,
    wave_index,
    radial_weight,
    ewald_mix,
    msg_weight,
    ewald_weight,
    out_weight,
):
    cx, cy, cz, slots, feat = features.shape
    levels, heads = radial_weight.shape
    cells = cx * cy * cz
    grid = [lax.axis_size("gx") * cx, lax.axis_size("gy") * cy, lax.axis_size("gz") * cz]
    devices = lax.axis_size("gx") * lax.axis_size("gy") * lax.axis_size("gz")
    waves = wave_index.shape[1]
    axes = ("gx", "gy", "gz")
    full = lambda shape: pl.BlockSpec(shape, lambda i: (0,) * len(shape))
    params = pltpu.CompilerParams(dimension_semantics=("arbitrary",), vmem_limit_bytes=56 * 2**20)

    masked = features * occupied[..., None].astype(jnp.bfloat16)
    frac = fractions.astype(jnp.float32)
    cell_feat = masked.reshape(cells, slots, feat)
    home = jnp.concatenate([frac, occupied[:, :, :, None, :].astype(jnp.float32)], axis=3)
    home = jnp.swapaxes(home.reshape(cells, 4, slots), 1, 2)

    start = [
        (lax.axis_index(n) * c + jnp.arange(c, dtype=jnp.int32)).astype(jnp.float32)
        for n, c in zip(axes, (cx, cy, cz))
    ]
    origin = jnp.stack(jnp.meshgrid(*start, indexing="ij"), axis=-1)[..., None]
    pos = (origin + frac).reshape(cells, 3, slots)
    lengths = jnp.array(grid, jnp.float32)
    index = wave_index.astype(jnp.float32)
    wave_vec = 2.0 * math.pi * index / lengths[:, None]
    wave_sq = jnp.sum(wave_vec * wave_vec, axis=0)
    damping = (
        strength
        * jnp.exp(-0.5 * smearing * wave_sq)
        / (wave_sq + screening)
        * (1.0 / math.sqrt(cells * slots * devices * waves))
    )
    wave_turn = (index / lengths[:, None]).T

    fold_z = grid[2] == 2 and cz == 1
    level = jnp.arange(levels, dtype=jnp.float32) / (levels - 1)
    wb = radial_weight * (jnp.exp(-sharpness * level * level) / math.sqrt(4.0 * slots))[:, None]
    wb = jnp.repeat(wb, feat // heads, axis=1)
    counts = tuple(lax.axis_size(n) for n in axes)
    rows = waves // devices
    chips = counts[0] * counts[1]
    if fold_z and rows % 16 == 0 and min(counts) > 1:
        spread = jnp.concatenate([fractions, occupied[:, :, :, None, :].astype(jnp.bfloat16)], axis=3)
        spread = jnp.pad(spread, ((0, 0),) * 3 + ((0, 12), (0, feat - slots)))
        pack = jnp.concatenate([features, spread], axis=3).reshape(cx, cy, slots + 16, feat)
        damp = lax.dynamic_slice_in_dim(damping, lax.axis_index(axes) * rows, rows, 0)
        damp = jnp.concatenate([damp, damp]).reshape(2 * rows, 1)
        vmem = pl.BlockSpec(memory_space=pltpu.VMEM)
        dma = pltpu.SemaphoreType.DMA
        out = pl.pallas_call(
            functools.partial(layer_kernel, counts, levels),
            in_specs=[vmem] * 10,
            out_specs=vmem,
            out_shape=jax.ShapeDtypeStruct((cells, slots, feat), jnp.bfloat16),
            scratch_shapes=[
                pltpu.VMEM((cx + 2, cy + 2, 2, slots + 16, feat), jnp.bfloat16),
                pltpu.VMEM((3, slots, slots), jnp.float32),
                pltpu.VMEM((3, levels * slots, 6 * slots), jnp.bfloat16),
                pltpu.VMEM((levels * slots, feat), jnp.float32),
                pltpu.VMEM((2 * waves, cells * slots), jnp.bfloat16),
                pltpu.VMEM((2, chips, 2, rows, feat), jnp.bfloat16),
                pltpu.VMEM((2, chips, rows, feat), jnp.bfloat16),
                pltpu.VMEM((2, chips, rows, feat), jnp.bfloat16),
                pltpu.VMEM((chips, 2, rows, feat), jnp.bfloat16),
                pltpu.VMEM((2, rows, feat), jnp.bfloat16),
                pltpu.VMEM((2, chips, 2, rows, feat), jnp.bfloat16),
                pltpu.VMEM((cells, slots, feat), jnp.bfloat16),
                dma((8,)),
                dma((8,)),
                dma((9,)),
                dma((9,)),
                dma,
                dma((2,)),
                dma((2,)),
                dma((chips,)),
                dma((chips,)),
                dma((chips,)),
                dma((chips,)),
            ],
            compiler_params=pltpu.CompilerParams(
                collective_id=0, has_side_effects=True, vmem_limit_bytes=56 * 2**20
            ),
            name="layer",
        )(pack, home, pos, wave_turn, wb, damp, ewald_mix, ewald_weight, msg_weight, out_weight)
        return out.reshape(features.shape)

    basis, struct = pl.pallas_call(
        basis_kernel,
        grid=(cells,),
        in_specs=[
            pl.BlockSpec((1, 3, slots), lambda i: (i, 0, 0)),
            full((waves, 3)),
            pl.BlockSpec((1, slots, feat), lambda i: (i, 0, 0)),
        ],
        out_specs=[pl.BlockSpec((1, 2 * waves, slots), lambda i: (i, 0, 0)), full((2 * waves, feat))],
        out_shape=[
            jax.ShapeDtypeStruct((cells, 2 * waves, slots), jnp.bfloat16),
            jax.ShapeDtypeStruct((2 * waves, feat), jnp.float32),
        ],
        compiler_params=params,
        name="basis",
    )(pos, wave_turn, cell_feat)

    wave_share = lax.psum_scatter(struct.reshape(2, waves, feat), axes, scatter_dimension=1, tiled=True)
    share_rows = wave_share.shape[1]
    share_damp = lax.dynamic_slice_in_dim(damping, lax.axis_index(axes) * share_rows, share_rows, 0)
    mixed = jnp.dot(wave_share.reshape(2 * share_rows, feat), ewald_mix, precision=lax.Precision.HIGHEST)
    filtered = (mixed.reshape(2, share_rows, feat) * share_damp[None, :, None]).astype(jnp.bfloat16)
    projected = jnp.dot(filtered, ewald_weight, preferred_element_type=jnp.float32).astype(jnp.bfloat16)
    field = lax.all_gather(projected, axes, axis=1, tiled=True).reshape(2 * waves, feat)

    wide_feat = widen(widen(masked, "gx", 0), "gy", 1)
    wide_geom = widen(widen(fractions, "gx", 0), "gy", 1)
    if fold_z:
        swap = [(0, 1), (1, 0)]
        wide_feat = jnp.concatenate([wide_feat, lax.ppermute(wide_feat, "gz", swap)], axis=2)
        wide_geom = jnp.concatenate([wide_geom, lax.ppermute(wide_geom, "gz", swap)], axis=2)
        near_z = 2
    else:
        wide_feat = widen(wide_feat, "gz", 2)
        wide_geom = widen(wide_geom, "gz", 2)
        near_z = 3
    wide_feat = jnp.stack([wide_feat[:, :, z : z + near_z] for z in range(cz)], axis=1)
    wide_geom = jnp.stack([wide_geom[:, :, z : z + near_z] for z in range(cz)], axis=1).astype(jnp.float32)
    messages = pl.pallas_call(
        functools.partial(message_kernel, cy, cz, fold_z, levels),
        grid=(cells,),
        in_specs=[
            pl.BlockSpec((1, slots, 4), lambda i: (i, 0, 0)),
            full(wide_feat.shape),
            full(wide_geom.shape),
            full(wb.shape),
        ],
        out_specs=pl.BlockSpec((1, slots, feat), lambda i: (i, 0, 0)),
        out_shape=jax.ShapeDtypeStruct((cells, slots, feat), jnp.bfloat16),
        scratch_shapes=[
            pltpu.VMEM((3, slots, slots), jnp.float32),
            pltpu.VMEM((3, levels * slots, 3 * near_z * slots), jnp.bfloat16),
            pltpu.VMEM((levels * slots, feat), jnp.float32),
        ],
        compiler_params=params,
        cost_estimate=pl.CostEstimate(
            flops=2 * cells * levels * slots * 9 * near_z * slots * feat, bytes_accessed=2**22, transcendentals=0
        ),
        name="messages",
    )(home, wide_feat, wide_geom, wb)

    out = pl.pallas_call(
        final_kernel,
        grid=(cells,),
        in_specs=[
            pl.BlockSpec((1, 2 * waves, slots), lambda i: (i, 0, 0)),
            full((2 * waves, feat)),
            pl.BlockSpec((1, slots, feat), lambda i: (i, 0, 0)),
            pl.BlockSpec((1, slots, feat), lambda i: (i, 0, 0)),
            pl.BlockSpec((1, slots, 4), lambda i: (i, 0, 0)),
            full((feat, feat)),
            full((feat, feat)),
        ],
        out_specs=pl.BlockSpec((1, slots, feat), lambda i: (i, 0, 0)),
        out_shape=jax.ShapeDtypeStruct((cells, slots, feat), jnp.bfloat16),
        compiler_params=params,
        name="final",
    )(basis, field, messages, cell_feat, home, msg_weight, out_weight)
    return out.reshape(features.shape)


def solution(mesh):
    cell = P("gx", "gy", "gz", None, None)
    in_specs = (cell, cell, P("gx", "gy", "gz", None), P(), P(), P(), P(), P(), P())
    return jax.shard_map(body, mesh=mesh, in_specs=in_specs, out_specs=cell, check_vma=False)
```
